32 devices in a mesh: row: 4 (over y, core), col: 8 (over z, x).
Axes of the slice: x: 2, y: 2, z: 4, core: 2. Of those that a mesh axis runs over, the one named last changes fastest.
Arguments:
- positions: float32 [3, 8192], P(None, 'col'), may hold values from 0 to 4
- modulus: float32 [8192], P('col'), may hold values from 0.5 to 2
- self_weight: float32 [64, 768], P('col'), may hold values from 1 to 4
- omega: float32 [64, 768, 256], P('col'), may hold values from -6 to 6
- psi: float32 [64, 768, 256], P('row'), may hold values from -6 to 6
- blocks: int32 [4, 8, 2, 2], P('row', 'col'), may hold values from -1 to 15, as said below
Outputs:
- row_basis: float32 [64, 768, 256], P('row', 'col')
- col_basis: float32 [64, 768, 256], P('col', 'row')
The draws below stay inside these ranges and needn't reach their ends.
Inputs may be any that keep to these rules, and one draw needn't show every extreme that they name: `blocks`: on every device the valid slots come first and the rest hold -1 in both entries; valid pairs are distinct, a row entry below 16, a column entry below 8, and never a cluster paired with itself; each device has at least one valid slot and some device has all 2 slots valid.
All inputs are finite; a program needn't handle non-finite values.
Results may differ from the reference program's by a relative error of at most 0.0003.
Values sent between devices are 32-bit elements; how exact they have to be, the bound alone decides.
A program may use at most 192 MiB of HBM per device.

```python
import math
import jax
import jax.numpy as jnp
from jax import lax

ZC = 128
SK = 256
CL_DEV = 8
BLK_DEV = 2
CLUSTERS = 64
ROW_CL = 16
ZONES = 8192
N_ROW = 4
N_COL = 8


def draw_blocks(key, part):
    row_count = CL_DEV * N_COL // N_ROW
    col_count = CL_DEV
    devices = N_ROW * N_COL
    pair_total = row_count * col_count
    key_score = jax.random.fold_in(key, 11)
    key_light = jax.random.fold_in(key, 12)
    key_heavy = jax.random.fold_in(key, 13)
    key_full = jax.random.fold_in(key, 14)
    scores = jax.random.randint(key_score, (devices, pair_total), 0, 2 ** 20) * pair_total + jnp.arange(pair_total, dtype=jnp.int32)[None, :]
    device_ids = jnp.arange(devices, dtype=jnp.int32)
    row_dev = device_ids // N_COL
    col_dev = device_ids % N_COL
    pair_ids = jnp.arange(pair_total, dtype=jnp.int32)
    global_row = row_dev[:, None] * row_count + pair_ids[None, :] // col_count
    global_col = col_dev[:, None] * col_count + pair_ids[None, :] % col_count
    scores = jnp.where(global_row == global_col, -1, scores)
    _, chosen = lax.top_k(scores, BLK_DEV)
    light = jax.random.randint(key_light, (devices,), 1, BLK_DEV // 2 + 1)
    heavy = jax.random.randint(key_heavy, (devices,), 0, 8) == 0
    full_one = jax.random.randint(key_full, (), 0, devices)
    counts = jnp.where(heavy | (device_ids == full_one), BLK_DEV, light)
    slot_ids = jnp.arange(BLK_DEV, dtype=jnp.int32)
    live = slot_ids[None, :] < counts[:, None]
    rows_local = jnp.where(live, chosen // col_count, -1)
    cols_local = jnp.where(live, chosen % col_count, -1)
    return jnp.stack([rows_local, cols_local], axis=-1).reshape(N_ROW, N_COL, BLK_DEV, 2).astype(jnp.int32)


def block_scale(own_key, extent, pieces, smallest, high):
    level = 1.0
    for position, parts in pieces:
        steps = jax.random.uniform(jax.random.fold_in(jax.random.fold_in(own_key, 6), position), (parts,), jnp.float32, smallest / len(pieces), high / len(pieces))
        level = level * jnp.repeat(jnp.exp(steps), extent[position] // parts).reshape((-1,) + (1,) * (len(extent) - 1 - position))
    return level


def bell_draw(rng, dims, scale, most, split=(), kind=jnp.bfloat16):
    entries = scale * jax.random.normal(rng, dims, jnp.float32)
    if split:
        entries = entries * block_scale(rng, dims, split, -0.22, 0.18)
    return jnp.clip(entries, -most, most).astype(kind)


def setup_inputs(seed: int = 0) -> dict:
    keys = jax.random.split(jax.random.key(seed), 7)
    positions = jnp.clip(4.0 * jax.random.uniform(keys[0], (3, ZONES), jnp.float32) ** block_scale(keys[0], (3, ZONES), ((1, 8),), -0.2, 0.2), 0.0, 4.0)
    modulus = jnp.clip(jnp.exp(math.log(2.0) - 1.3862944 * jax.random.uniform(keys[1], (ZONES,), jnp.float32) ** block_scale(keys[1], (ZONES,), ((0, 8),), -0.2, 0.2)), 0.5, 2.0)
    self_weight = jnp.clip(jnp.exp(math.log(4.0) - 1.3862944 * jax.random.uniform(keys[2], (CLUSTERS, 6 * ZC), jnp.float32) ** block_scale(keys[2], (CLUSTERS, 6 * ZC), ((0, 8),), -0.2, 0.2)), 1.0, 4.0)
    omega = bell_draw(keys[3], (CLUSTERS, 6 * ZC, SK), 1.0, 6.0, ((0, 8),), jnp.float32)
    psi = bell_draw(keys[4], (CLUSTERS, 6 * ZC, SK), 1.0, 6.0, ((0, 4),), jnp.float32)
    blocks = draw_blocks(jax.random.fold_in(keys[6], 71), 0)
    return {"positions": positions, "modulus": modulus, "self_weight": self_weight, "omega": omega, "psi": psi, "blocks": blocks}


COUPLE = 0.25
ROOT_TWO = 1.4142135623730951
HIGH = lax.Precision.HIGHEST

def make_tiles(row_points, row_scale, col_points, col_scale):
    offsets = row_points[:, :, :, None] - col_points[:, :, None, :]
    spread = lax.optimization_barrier(jnp.sum(offsets * offsets, axis=1)) + 1.0
    inverse = lax.rsqrt(spread)
    normal = offsets * inverse[:, None]
    weight_ab = COUPLE * inverse * inverse * inverse * row_scale[:, :, None] * col_scale[:, None, :]
    comp_x = normal[:, 0]
    comp_y = normal[:, 1]
    comp_z = normal[:, 2]
    voigt = jnp.stack([comp_x * comp_x, comp_y * comp_y, comp_z * comp_z, ROOT_TWO * comp_y * comp_z, ROOT_TWO * comp_x * comp_z, ROOT_TWO * comp_x * comp_y], axis=1)
    trace_vec = jnp.array([1.0, 1.0, 1.0, 0.0, 0.0, 0.0], dtype=voigt.dtype)
    identity = jnp.eye(6, dtype=voigt.dtype)
    voigt_row = voigt[:, :, :, None, :]
    voigt_col = jnp.transpose(voigt, (0, 2, 1, 3))[:, None]
    angular = identity[None, :, None, :, None] + voigt_row * trace_vec[None, None, None, :, None] + trace_vec[None, :, None, None, None] * voigt_col - 5.0 * voigt_row * voigt_col
    result = angular * weight_ab[:, None, :, None, :]
    zones_per = row_points.shape[2]
    return result.reshape(result.shape[0], 6 * zones_per, 6 * zones_per)

def orthonormal(sketch):
    gram = jnp.einsum('kxs,kxt->kst', sketch, sketch, precision=HIGH)
    factor = jnp.linalg.cholesky(gram)
    return lax.linalg.triangular_solve(factor, sketch, left_side=False, lower=True, transpose_a=True)

def reference(positions, modulus, self_weight, omega, psi, blocks):
    points = positions.reshape(3, CLUSTERS, ZC)
    scales = modulus.reshape(CLUSTERS, ZC)
    row_base = (jnp.arange(N_ROW, dtype=jnp.int32) * ROW_CL)[:, None, None]
    col_base = (jnp.arange(N_COL, dtype=jnp.int32) * CL_DEV)[None, :, None]
    valid = blocks[..., 0] >= 0
    row_ids = jnp.where(valid, row_base + blocks[..., 0], 0).reshape(-1).astype(jnp.int32)
    col_ids = jnp.where(valid, col_base + blocks[..., 1], 0).reshape(-1).astype(jnp.int32)
    flags = valid.reshape(-1)
    start_rows = self_weight[:, :, None] * omega
    start_cols = self_weight[:, :, None] * psi

    def visit(state, entry):
        row_id, col_id, flag = entry

        def add_pair(inner):
            sketch_rows, sketch_cols = inner
            row_pts = lax.dynamic_index_in_dim(points, row_id, 1, keepdims=False)
            col_pts = lax.dynamic_index_in_dim(points, col_id, 1, keepdims=False)
            row_mod = lax.dynamic_index_in_dim(scales, row_id, 0, keepdims=False)
            col_mod = lax.dynamic_index_in_dim(scales, col_id, 0, keepdims=False)
            block = make_tiles(row_pts[None], row_mod[None], col_pts[None], col_mod[None])[0]
            omega_j = lax.dynamic_index_in_dim(omega, col_id, 0, keepdims=False)
            psi_i = lax.dynamic_index_in_dim(psi, row_id, 0, keepdims=False)
            row_term = jnp.dot(block, omega_j, precision=HIGH)
            col_term = jnp.dot(block.T, psi_i, precision=HIGH)
            return (sketch_rows.at[row_id].add(row_term), sketch_cols.at[col_id].add(col_term))
        return (lax.cond(flag, add_pair, lambda inner: inner, state), None)
    (row_sketch, col_sketch), _ = lax.scan(visit, (start_rows, start_cols), (row_ids, col_ids, flags))
    return (orthonormal(row_sketch), orthonormal(col_sketch))
```

```python
import functools

import jax
import jax.numpy as jnp
from jax import lax
from jax.experimental import pallas as pl
from jax.experimental.pallas import tpu as pltpu
from jax.sharding import PartitionSpec as P

COUPLE = 0.25
ROOT_TWO = 1.4142135623730951
HIGH = lax.Precision.HIGHEST
BASE = 64
LANES = 128
MESH = pl.DeviceIdType.MESH
ANY = pl.BlockSpec(memory_space=pl.ANY)


def exchange(outgoing, incoming, barrier, send_sem, recv_sem, local_sem):
    row = lax.axis_index("row")
    col = lax.axis_index("col")
    remote_out = jnp.int32(0)
    for _, device, _, cond in incoming:
        here = jnp.logical_and(device[0] == row, device[1] == col)

        @pl.when(jnp.logical_and(cond, jnp.logical_not(here)))
        def _():
            pl.semaphore_signal(barrier, inc=1, device_id=device, device_id_type=MESH)

    for _, _, device, _, cond in outgoing:
        here = jnp.logical_and(device[0] == row, device[1] == col)
        remote_out = remote_out + jnp.logical_and(cond, jnp.logical_not(here)).astype(jnp.int32)
    pl.semaphore_wait(barrier, remote_out)

    def each_out(action):
        for number, (src, dst, device, slot, cond) in enumerate(outgoing):
            here = jnp.logical_and(device[0] == row, device[1] == col)
            remote = pltpu.make_async_remote_copy(
                src_ref=src,
                dst_ref=dst,
                send_sem=send_sem.at[number],
                recv_sem=recv_sem.at[slot],
                device_id=device,
                device_id_type=MESH,
            )
            local = pltpu.make_async_copy(src, dst, local_sem.at[number])

            @pl.when(jnp.logical_and(cond, jnp.logical_not(here)))
            def _():
                remote.start() if action == "start" else remote.wait_send()

            @pl.when(jnp.logical_and(cond, here))
            def _():
                local.start() if action == "start" else local.wait()

    each_out("start")
    for dst, device, slot, cond in incoming:
        here = jnp.logical_and(device[0] == row, device[1] == col)

        @pl.when(jnp.logical_and(cond, jnp.logical_not(here)))
        def _():
            pltpu.make_async_remote_copy(
                src_ref=dst,
                dst_ref=dst,
                send_sem=send_sem.at[0],
                recv_sem=recv_sem.at[slot],
                device_id=device,
                device_id_type=MESH,
            ).wait_recv()

    each_out("wait")


def remote_call(body, out_shapes, sems_out, sems_in, ident, operands):
    return pl.pallas_call(
        body,
        out_shape=out_shapes,
        in_specs=[ANY] * len(operands),
        out_specs=[ANY] * len(out_shapes),
        scratch_shapes=[
            pltpu.SemaphoreType.DMA((sems_out,)),
            pltpu.SemaphoreType.DMA((sems_in,)),
            pltpu.SemaphoreType.DMA((sems_out,)),
        ],
        compiler_params=pltpu.CompilerParams(collective_id=ident, has_side_effects=True),
        name="exchange_%d" % ident,
    )(*operands)


def f32(*shape):
    return jax.ShapeDtypeStruct(shape, jnp.float32)


def gather_kernel(sizes, points_ref, meta_ref, out_points, out_meta, send_sem, recv_sem, local_sem):
    n_row, n_col, ratio = sizes
    row = lax.axis_index("row")
    col = lax.axis_index("col")
    yes = jnp.bool_(True)
    outgoing, incoming = [], []
    owner_here = col // ratio == row
    for c in range(n_col):
        outgoing.append((points_ref, out_points.at[lax.rem(col, ratio)], (row, c), lax.rem(col, ratio), owner_here))
    for x in range(ratio):
        incoming.append((out_points.at[x], (row, row * ratio + x), x, yes))
    for q in range(n_col):
        outgoing.append(
            (meta_ref, out_meta.at[col], (q // ratio, row * ratio + q % ratio), ratio + col, yes)
        )
        incoming.append((out_meta.at[q], (col // ratio, q), ratio + q, yes))
    for p in range(n_row):
        outgoing.append((meta_ref, out_meta.at[n_col + row], (p, col), ratio + n_col + row, yes))
        incoming.append((out_meta.at[n_col + p], (p, col), ratio + n_col + p, yes))
    exchange(outgoing, incoming, pltpu.get_barrier_semaphore(), send_sem, recv_sem, local_sem)


def spread_kernel(
    sizes, row_terms, col_terms, psi, out_rows, out_cols, out_psi, send_sem, recv_sem, local_sem
):
    n_row, n_col, ratio, own = sizes
    row = lax.axis_index("row")
    col = lax.axis_index("col")
    yes = jnp.bool_(True)
    row_part = row_terms.shape[1] // n_col
    col_part = col_terms.shape[1] // n_row
    outgoing, incoming = [], []
    for q in range(n_col):
        outgoing.append(
            (
                row_terms.at[:, q * row_part : (q + 1) * row_part],
                out_rows.at[col],
                (q // ratio, row * ratio + q % ratio),
                col,
                yes,
            )
        )
        incoming.append((out_rows.at[q], (col // ratio, q), q, yes))
    for p in range(n_row):
        outgoing.append(
            (col_terms.at[:, p * col_part : (p + 1) * col_part], out_cols.at[row], (p, col), n_col + row, yes)
        )
        incoming.append((out_cols.at[p], (p, col), n_col + p, yes))
    has_psi = col // ratio == row
    first = lax.rem(col, ratio) * (own * n_row)
    for p in range(n_row):
        outgoing.append((psi.at[pl.ds(first + p * own, own)], out_psi, (p, col), n_col + n_row, has_psi))
    incoming.append((out_psi, (col // ratio, col), n_col + n_row, yes))
    exchange(outgoing, incoming, pltpu.get_barrier_semaphore(), send_sem, recv_sem, local_sem)


def collect_kernel(sizes, rows, cols, out_rows, out_cols, send_sem, recv_sem, local_sem):
    n_row, n_col, ratio, own = sizes
    row = lax.axis_index("row")
    col = lax.axis_index("col")
    yes = jnp.bool_(True)
    group = col // ratio
    mine = row * ratio + lax.rem(col, ratio)
    outgoing, incoming = [], []
    for q in range(n_col):
        device = (q // ratio, group * ratio + q % ratio)
        start = (q % ratio) * (own * n_row) + (q // ratio) * own
        outgoing.append((rows.at[pl.ds(start, own)], out_rows.at[mine], device, mine, yes))
        incoming.append((out_rows.at[q], device, q, yes))
    for p in range(n_row):
        outgoing.append((cols.at[pl.ds(p * own, own)], out_cols.at[row], (p, col), n_col + row, yes))
        incoming.append((out_cols.at[p], (p, col), n_col + p, yes))
    exchange(outgoing, incoming, pltpu.get_barrier_semaphore(), send_sem, recv_sem, local_sem)


def deliver_kernel(sizes, rows, cols, out_rows, out_cols, send_sem, recv_sem, local_sem):
    n_row, n_col, ratio, own = sizes
    row = lax.axis_index("row")
    col = lax.axis_index("col")
    yes = jnp.bool_(True)
    row_part = rows.shape[1] // n_col
    col_part = cols.shape[1] // n_row
    outgoing, incoming = [], []
    mine = row * ratio + lax.rem(col, ratio)
    place = lax.rem(col, ratio) * (own * n_row) + row * own
    for c in range(n_col):
        outgoing.append(
            (
                rows.at[:, c * row_part : (c + 1) * row_part],
                out_rows.at[pl.ds(place, own)],
                (col // ratio, c),
                mine,
                yes,
            )
        )
        start = (c % ratio) * (own * n_row) + (c // ratio) * own
        incoming.append((out_rows.at[pl.ds(start, own)], (c // ratio, row * ratio + c % ratio), c, yes))
    for p in range(n_row):
        outgoing.append(
            (
                cols.at[:, p * col_part : (p + 1) * col_part],
                out_cols.at[pl.ds(row * own, own)],
                (p, col),
                n_col + row,
                yes,
            )
        )
        incoming.append((out_cols.at[pl.ds(p * own, own)], (p, col), n_col + p, yes))
    exchange(outgoing, incoming, pltpu.get_barrier_semaphore(), send_sem, recv_sem, local_sem)


def dot(a, b, contract):
    return lax.dot_general(
        a, b, (contract, ((), ())), precision=HIGH, preferred_element_type=jnp.float32
    )


def terms_kernel(pairs, left_ref, right_ref, omega_ref, psi_ref, row_ref, col_ref):
    slot = pl.program_id(0)
    live = pairs[slot, 0] >= 0
    zones = right_ref.shape[2]

    @pl.when(jnp.logical_not(live))
    def _():
        row_ref[...] = jnp.zeros_like(row_ref)
        col_ref[...] = jnp.zeros_like(col_ref)

    @pl.when(live)
    def _():
        offs = [left_ref[0, :, n : n + 1] - right_ref[0, n : n + 1, :] for n in range(3)]
        spread = (offs[0] * offs[0] + offs[1] * offs[1] + offs[2] * offs[2]) + 1.0
        inverse = lax.rsqrt(spread)
        nx, ny, nz = [o * inverse for o in offs]
        weight = COUPLE * inverse * inverse * inverse * left_ref[0, :, 3:4] * right_ref[0, 3:4, :]
        u = [nx * nx, ny * ny, nz * nz, ROOT_TWO * ny * nz, ROOT_TWO * nx * nz, ROOT_TWO * nx * ny]
        for p in range(6):
            parts = []
            for q in range(6):
                val = -5.0 * u[p] * u[q]
                if q < 3:
                    val = val + u[p]
                if p < 3:
                    val = val + u[q]
                if p == q:
                    val = val + 1.0
                parts.append(weight * val)
            strip = jnp.concatenate(parts, axis=1)
            span = slice(p * zones, (p + 1) * zones)
            row_ref[0, span, :] = dot(strip, omega_ref[0], ((1,), (0,)))
            term = dot(strip, psi_ref[0, span, :], ((0,), (0,)))
            if p == 0:
                col_ref[0] = term
            else:
                col_ref[0] += term


def add_kernel(ids, terms_ref, out_ref):
    count = terms_ref.shape[0]
    slots = terms_ref.shape[1]
    out_ref[...] = jnp.zeros_like(out_ref)

    @pl.loop(0, count * slots)
    def _(n):
        target = ids[n]

        @pl.when(target >= 0)
        def _():
            out_ref[target] += terms_ref[n // slots, n % slots]


def sum_terms(terms, ids, clusters):
    part = terms.shape[2]
    width = terms.shape[3]
    return pl.pallas_call(
        add_kernel,
        out_shape=f32(clusters, part, width),
        grid_spec=pltpu.PrefetchScalarGridSpec(
            num_scalar_prefetch=1,
            grid=(1,),
            in_specs=[pl.BlockSpec(terms.shape, lambda n, _: (0, 0, 0, 0), pipeline_mode=pl.Buffered(1))],
            out_specs=pl.BlockSpec((clusters, part, width), lambda n, _: (0, 0, 0), pipeline_mode=pl.Buffered(1)),
        ),
        name="sum_terms",
    )(ids, terms)


def invert_base(blocks):
    size = blocks[0].shape[0]
    rows = lax.broadcasted_iota(jnp.int32, (size, size), 0)
    cols = lax.broadcasted_iota(jnp.int32, (size, size), 1)
    eye = (rows == cols).astype(jnp.float32)
    work = [jnp.concatenate([b, eye], axis=1) for b in blocks]
    done = [[] for _ in blocks]
    for k in range(size):
        low = (k // 8) * 8
        nxt = []
        for m, w in enumerate(work):
            at = k - low
            pivot_row = w[at : at + 1, :]
            d = pivot_row[:, k : k + 1]
            root = lax.rsqrt(d)
            scaled = pivot_row * root
            done[m].append(scaled[:, size:])
            if k + 1 < size:
                column = w[:, k : k + 1] * root
                if at == 7:
                    nxt.append(w[8:] - column[8:] * scaled)
                else:
                    nxt.append(w - column * scaled)
        work = nxt
    return [jnp.concatenate(d, axis=0) for d in done]


def basis_kernel(own, row_terms, col_terms, omega_ref, psi_ref, weight_ref, row_ref, col_ref, aug):
    width = omega_ref.shape[2]
    for k in range(own):
        for terms, start, out in ((row_terms, omega_ref, row_ref), (col_terms, psi_ref, col_ref)):
            pieces = terms.shape[0]
            part = terms.shape[2]
            for c in range(pieces):
                span = slice(c * part, (c + 1) * part)
                out[k, span, :] = weight_ref[k, span, :] * start[k, span, :] + terms[c, k]
    rows = lax.broadcasted_iota(jnp.int32, (width, width), 0)
    cols = lax.broadcasted_iota(jnp.int32, (width, width), 1)
    eye = (rows == cols).astype(jnp.float32)
    sources = [(out, k) for k in range(own) for out in (row_ref, col_ref)]
    for m, (out, k) in enumerate(sources):
        aug[m, :, :width] = dot(out[k], out[k], ((0,), (0,)))
        aug[m, :, width:] = eye
    steps = width // BASE
    lane = lax.broadcasted_iota(jnp.int32, (BASE, width), 1)
    for s in range(steps):
        span = slice(s * BASE, (s + 1) * BASE)
        inverses = invert_base([aug[m, span, span] for m in range(len(sources))])
        for m in range(len(sources)):
            panel = dot(inverses[m], aug[m, span, :], ((1,), (0,)))
            aug[m, span, :] = panel
            if s + 1 < steps:
                rest = slice((s + 1) * BASE, width)
                update = dot(jnp.where(lane >= (s + 1) * BASE, panel[:, :width], 0.0), panel, ((0,), (0,)))
                aug[m, rest, :] = aug[m, rest, :] - update[(s + 1) * BASE :]
    for m, (out, k) in enumerate(sources):
        out[k] = dot(out[k], aug[m, :, width:], ((1,), (1,)))


def per_device(positions, modulus, self_weight, omega, psi, blocks, *, n_row, n_col):
    col_clusters, height, width = omega.shape
    row_clusters = psi.shape[0]
    zones = positions.shape[1] // col_clusters
    ratio = row_clusters // col_clusters
    own = col_clusters // n_row
    row = lax.axis_index("row")
    col = lax.axis_index("col")
    pairs = blocks.reshape(-1, 2)
    slots = pairs.shape[0]

    points = jnp.concatenate([positions, modulus[None]], axis=0)
    meta = jnp.pad(pairs.astype(jnp.float32).reshape(1, -1), ((0, 7), (0, LANES - 2 * slots)))
    all_points, all_meta = remote_call(
        functools.partial(gather_kernel, (n_row, n_col, ratio)),
        [f32(ratio, 4, positions.shape[1]), f32(n_col + n_row, 8, LANES)],
        2 * n_col + n_row,
        ratio + n_col + n_row,
        1,
        [points, meta],
    )
    row_points = all_points.reshape(ratio, 4, col_clusters, zones).transpose(0, 2, 3, 1)
    row_points = row_points.reshape(row_clusters, zones, 4)
    col_points = points.reshape(4, col_clusters, zones).transpose(1, 0, 2)
    metas = all_meta[:, 0, : 2 * slots].astype(jnp.int32).reshape(n_col + n_row, slots, 2)
    row_ids = metas[:n_col, :, 0].reshape(-1)
    col_ids = metas[n_col:, :, 1].reshape(-1)

    row_terms, col_terms = pl.pallas_call(
        terms_kernel,
        out_shape=[f32(slots, height, width), f32(slots, height, width)],
        grid_spec=pltpu.PrefetchScalarGridSpec(
            num_scalar_prefetch=1,
            grid=(slots,),
            in_specs=[
                pl.BlockSpec((1, zones, 4), lambda n, ids: (jnp.maximum(ids[n, 0], 0), 0, 0)),
                pl.BlockSpec((1, 4, zones), lambda n, ids: (jnp.maximum(ids[n, 1], 0), 0, 0)),
                pl.BlockSpec((1, height, width), lambda n, ids: (jnp.maximum(ids[n, 1], 0), 0, 0)),
                pl.BlockSpec((1, height, width), lambda n, ids: (jnp.maximum(ids[n, 0], 0), 0, 0)),
            ],
            out_specs=[
                pl.BlockSpec((1, height, width), lambda n, ids: (n, 0, 0)),
                pl.BlockSpec((1, height, width), lambda n, ids: (n, 0, 0)),
            ],
        ),
        name="terms",
    )(pairs, row_points, col_points, omega, psi)

    sizes = (n_row, n_col, ratio, own)
    row_part = height // n_col
    col_part = height // n_row
    got_rows, got_cols, own_psi = remote_call(
        functools.partial(spread_kernel, sizes),
        [
            f32(n_col, slots, row_part, width),
            f32(n_row, slots, col_part, width),
            f32(own, height, width),
        ],
        n_col + 2 * n_row,
        n_col + n_row + 1,
        2,
        [row_terms, col_terms, psi],
    )
    row_chunks = sum_terms(got_rows, row_ids, row_clusters)
    col_chunks = sum_terms(got_cols, col_ids, col_clusters)
    full_rows, full_cols = remote_call(
        functools.partial(collect_kernel, sizes),
        [f32(n_col, own, row_part, width), f32(n_row, own, col_part, width)],
        n_col + n_row,
        n_col + n_row,
        3,
        [row_chunks, col_chunks],
    )
    own_omega = lax.dynamic_slice_in_dim(omega, row * own, own, 0)
    own_weight = lax.dynamic_slice_in_dim(self_weight, row * own, own, 0)[:, :, None]
    full = pl.BlockSpec(memory_space=pltpu.VMEM)
    row_basis, col_basis = pl.pallas_call(
        functools.partial(basis_kernel, own),
        out_shape=[f32(own, height, width), f32(own, height, width)],
        in_specs=[full] * 5,
        out_specs=[full] * 2,
        scratch_shapes=[pltpu.VMEM((2 * own, width, 2 * width), jnp.float32)],
        name="basis",
    )(full_rows, full_cols, own_omega, own_psi, own_weight)
    return tuple(
        remote_call(
            functools.partial(deliver_kernel, sizes),
            [f32(row_clusters, row_part, width), f32(col_clusters, col_part, width)],
            n_col + n_row,
            n_col + n_row,
            4,
            [row_basis, col_basis],
        )
    )


def solution(mesh):
    placed = (
        P(None, "col"),
        P("col"),
        P("col", None),
        P("col", None, None),
        P("row", None, None),
        P("row", "col", None, None),
    )
    return jax.shard_map(
        functools.partial(per_device, n_row=mesh.shape["row"], n_col=mesh.shape["col"]),
        mesh=mesh,
        in_specs=placed,
        out_specs=(P("row", "col", None), P("col", "row", None)),
        check_vma=False,
    )
```

```python
import functools
import math

import jax
import jax.numpy as jnp
from jax import lax
from jax.experimental import pallas as pl
from jax.experimental.pallas import tpu as pltpu
from jax.sharding import PartitionSpec as P

COUPLE = 0.25
ROOT_TWO = 1.4142135623730951
HIGH = lax.Precision.HIGHEST
BASE = 64
LANES = 128
MESH = pl.DeviceIdType.MESH
ANY = pl.BlockSpec(memory_space=pl.ANY)


def exchange(outgoing, incoming, barrier, send_sem, recv_sem, local_sem):
    row = lax.axis_index("row")
    col = lax.axis_index("col")
    remote_out = jnp.int32(0)
    for _, device, _, cond in incoming:
        here = jnp.logical_and(device[0] == row, device[1] == col)

        @pl.when(jnp.logical_and(cond, jnp.logical_not(here)))
        def _():
            pl.semaphore_signal(barrier, inc=1, device_id=device, device_id_type=MESH)

    for _, _, device, _, cond in outgoing:
        here = jnp.logical_and(device[0] == row, device[1] == col)
        remote_out = remote_out + jnp.logical_and(cond, jnp.logical_not(here)).astype(jnp.int32)
    pl.semaphore_wait(barrier, remote_out)

    def each_out(action):
        for number, (src, dst, device, slot, cond) in enumerate(outgoing):
            here = jnp.logical_and(device[0] == row, device[1] == col)
            remote = pltpu.make_async_remote_copy(
                src_ref=src,
                dst_ref=dst,
                send_sem=send_sem.at[number],
                recv_sem=recv_sem.at[slot],
                device_id=device,
                device_id_type=MESH,
            )
            local = pltpu.make_async_copy(src, dst, local_sem.at[number])

            @pl.when(jnp.logical_and(cond, jnp.logical_not(here)))
            def _():
                remote.start() if action == "start" else remote.wait_send()

            @pl.when(jnp.logical_and(cond, here))
            def _():
                local.start() if action == "start" else local.wait()

    each_out("start")
    for dst, device, slot, cond in incoming:
        here = jnp.logical_and(device[0] == row, device[1] == col)

        @pl.when(jnp.logical_and(cond, jnp.logical_not(here)))
        def _():
            pltpu.make_async_remote_copy(
                src_ref=dst,
                dst_ref=dst,
                send_sem=send_sem.at[0],
                recv_sem=recv_sem.at[slot],
                device_id=device,
                device_id_type=MESH,
            ).wait_recv()

    each_out("wait")


def remote_call(body, out_shapes, sems_out, sems_in, ident, operands):
    return pl.pallas_call(
        body,
        out_shape=out_shapes,
        in_specs=[ANY] * len(operands),
        out_specs=[ANY] * len(out_shapes),
        scratch_shapes=[
            pltpu.SemaphoreType.DMA((sems_out,)),
            pltpu.SemaphoreType.DMA((sems_in,)),
            pltpu.SemaphoreType.DMA((sems_out,)),
        ],
        compiler_params=pltpu.CompilerParams(collective_id=ident, has_side_effects=True),
        name="exchange_%d" % ident,
    )(*operands)


def f32(*shape):
    return jax.ShapeDtypeStruct(shape, jnp.float32)


def gather_kernel(sizes, points_ref, meta_ref, out_points, out_meta, send_sem, recv_sem, local_sem):
    n_row, n_col, ratio = sizes
    row = lax.axis_index("row")
    col = lax.axis_index("col")
    yes = jnp.bool_(True)
    outgoing, incoming = [], []
    for c in range(n_col):
        outgoing.append((points_ref, out_points.at[col], (row, c), col, yes))
        incoming.append((out_points.at[c], (row, c), c, yes))
    for q in range(n_col):
        outgoing.append(
            (meta_ref, out_meta.at[col], (q // ratio, row * ratio + q % ratio), n_col + col, yes)
        )
        incoming.append((out_meta.at[q], (col // ratio, q), n_col + q, yes))
    for p in range(n_row):
        outgoing.append((meta_ref, out_meta.at[n_col + row], (p, col), 2 * n_col + row, yes))
        incoming.append((out_meta.at[n_col + p], (p, col), 2 * n_col + p, yes))
    exchange(outgoing, incoming, pltpu.get_barrier_semaphore(), send_sem, recv_sem, local_sem)


def spread_kernel(sizes, row_terms, col_terms, out_rows, out_cols, send_sem, recv_sem, local_sem):
    n_row, n_col, ratio, own = sizes
    row = lax.axis_index("row")
    col = lax.axis_index("col")
    yes = jnp.bool_(True)
    row_part = out_rows.shape[2]
    col_part = out_cols.shape[2]
    outgoing, incoming = [], []
    for c in range(n_col):
        x = c % ratio
        outgoing.append(
            (
                row_terms.at[c // ratio, :, x * row_part : (x + 1) * row_part],
                out_rows.at[col],
                (row, c),
                col,
                yes,
            )
        )
        incoming.append((out_rows.at[c], (row, c), c, yes))
    for p in range(n_row):
        outgoing.append(
            (col_terms.at[:, p * col_part : (p + 1) * col_part], out_cols.at[row], (p, col), n_col + row, yes)
        )
        incoming.append((out_cols.at[p], (p, col), n_col + p, yes))
    exchange(outgoing, incoming, pltpu.get_barrier_semaphore(), send_sem, recv_sem, local_sem)


def collect_kernel(sizes, rows, cols, out_rows, out_cols, send_sem, recv_sem, local_sem):
    n_row, n_col, ratio, own = sizes
    row = lax.axis_index("row")
    col = lax.axis_index("col")
    yes = jnp.bool_(True)
    group = col // ratio
    mine = row * ratio + lax.rem(col, ratio)
    outgoing, incoming = [], []
    for q in range(n_col):
        device = (q // ratio, group * ratio + q % ratio)
        start = (q % ratio) * (own * n_row) + (q // ratio) * own
        outgoing.append((rows.at[pl.ds(start, own)], out_rows.at[mine], device, mine, yes))
        incoming.append((out_rows.at[q], device, q, yes))
    for p in range(n_row):
        outgoing.append((cols.at[pl.ds(p * own, own)], out_cols.at[row], (p, col), n_col + row, yes))
        incoming.append((out_cols.at[p], (p, col), n_col + p, yes))
    exchange(outgoing, incoming, pltpu.get_barrier_semaphore(), send_sem, recv_sem, local_sem)


def deliver_kernel(sizes, rows, cols, out_rows, out_cols, send_sem, recv_sem, local_sem):
    n_row, n_col, ratio, own = sizes
    row = lax.axis_index("row")
    col = lax.axis_index("col")
    yes = jnp.bool_(True)
    row_part = rows.shape[1] // n_col
    col_part = cols.shape[1] // n_row
    outgoing, incoming = [], []
    mine = row * ratio + lax.rem(col, ratio)
    place = lax.rem(col, ratio) * (own * n_row) + row * own
    for c in range(n_col):
        outgoing.append(
            (
                rows.at[:, c * row_part : (c + 1) * row_part],
                out_rows.at[pl.ds(place, own)],
                (col // ratio, c),
                mine,
                yes,
            )
        )
        start = (c % ratio) * (own * n_row) + (c // ratio) * own
        incoming.append((out_rows.at[pl.ds(start, own)], (c // ratio, row * ratio + c % ratio), c, yes))
    for p in range(n_row):
        outgoing.append(
            (
                cols.at[:, p * col_part : (p + 1) * col_part],
                out_cols.at[pl.ds(row * own, own)],
                (p, col),
                n_col + row,
                yes,
            )
        )
        incoming.append((out_cols.at[pl.ds(p * own, own)], (p, col), n_col + p, yes))
    exchange(outgoing, incoming, pltpu.get_barrier_semaphore(), send_sem, recv_sem, local_sem)


def dot(a, b, contract):
    return lax.dot_general(
        a, b, (contract, ((), ())), precision=HIGH, preferred_element_type=jnp.float32
    )


def upright(line):
    size = line.shape[1]
    return jnp.transpose(jnp.broadcast_to(line, (size, size)))


def shape_of(left, right_ref):
    offs = [left[n] - right_ref[n : n + 1, :] for n in range(3)]
    spread = (offs[0] * offs[0] + offs[1] * offs[1] + offs[2] * offs[2]) + 1.0
    inverse = lax.rsqrt(spread)
    nx, ny, nz = [o * inverse for o in offs]
    weight = COUPLE * inverse * inverse * inverse * left[3] * right_ref[3:4, :]
    u = [nx * nx, ny * ny, nz * nz, ROOT_TWO * ny * nz, ROOT_TWO * nx * nz, ROOT_TWO * nx * ny]
    return u, weight


def row_terms_kernel(ids, left_ref, right_ref, omega_ref, out_ref, held):
    n = pl.program_id(0)
    live = ids[n, 0] >= 0
    slab = ids[n, 2]
    zones = right_ref.shape[1]
    rows = out_ref.shape[1]
    step = math.gcd(zones, rows)
    per = zones // step

    @pl.when(jnp.logical_not(live))
    def _():
        out_ref[...] = jnp.zeros_like(out_ref)

    @pl.when(live)
    def _():
        for m in range(4):
            held[m] = upright(left_ref[0, m : m + 1, :])
        for g in range(rows // step):
            which = slab * (rows // step) + g
            p = which // per
            start = pl.multiple_of((which % per) * step, step)
            u, weight = shape_of([held[m, pl.ds(start, step), :] for m in range(4)], right_ref)
            mine = u[5]
            for k in range(5):
                mine = jnp.where(p == k, u[k], mine)
            trace = (p < 3).astype(jnp.float32)
            parts = []
            for q in range(6):
                val = trace * u[q] - 5.0 * mine * u[q] + (p == q).astype(jnp.float32)
                if q < 3:
                    val = val + mine
                parts.append(weight * val)
            strip = jnp.concatenate(parts, axis=1)
            out_ref[0, g * step : (g + 1) * step, :] = dot(strip, omega_ref[0], ((1,), (0,)))


def col_terms_kernel(ids, left_ref, right_ref, psi_ref, out_ref):
    n = pl.program_id(0)
    live = ids[n, 0] >= 0
    zones = right_ref.shape[1]

    @pl.when(jnp.logical_not(live))
    def _():
        out_ref[...] = jnp.zeros_like(out_ref)

    @pl.when(live)
    def _():
        left = [upright(right_ref[m : m + 1, :]) for m in range(4)]
        u, weight = shape_of(left, left_ref.at[0])
        for p in range(6):
            parts = []
            for q in range(6):
                val = -5.0 * u[p] * u[q]
                if q < 3:
                    val = val + u[p]
                if p < 3:
                    val = val + u[q]
                if p == q:
                    val = val + 1.0
                parts.append(weight * val)
            strip = jnp.concatenate(parts, axis=1)
            out_ref[0, p * zones : (p + 1) * zones, :] = dot(strip, psi_ref[0], ((1,), (0,)))


def add_kernel(row_ids, col_ids, rows_ref, cols_ref, out_rows, out_cols):
    for ids, terms_ref, out_ref in ((row_ids, rows_ref, out_rows), (col_ids, cols_ref, out_cols)):
        out_ref[...] = jnp.zeros_like(out_ref)
        slots = terms_ref.shape[1]

        @pl.loop(0, terms_ref.shape[0] * slots)
        def _(n):
            target = ids[n]

            @pl.when(target >= 0)
            def _():
                out_ref[target] += terms_ref[n // slots, n % slots]


def sum_terms(row_ids, col_ids, rows, cols, row_clusters, col_clusters):
    whole = pl.BlockSpec(memory_space=pltpu.VMEM)
    table = pl.BlockSpec(memory_space=pltpu.SMEM)
    return pl.pallas_call(
        add_kernel,
        out_shape=[f32(row_clusters, *rows.shape[2:]), f32(col_clusters, *cols.shape[2:])],
        in_specs=[table, table, whole, whole],
        out_specs=[whole, whole],
        name="sum_terms",
    )(row_ids, col_ids, rows, cols)


def invert_base(blocks):
    size = blocks[0].shape[0]
    rows = lax.broadcasted_iota(jnp.int32, (size, size), 0)
    cols = lax.broadcasted_iota(jnp.int32, (size, size), 1)
    eye = (rows == cols).astype(jnp.float32)
    work = [jnp.concatenate([b, eye], axis=1) for b in blocks]
    done = [[] for _ in blocks]
    for k in range(size):
        low = (k // 8) * 8
        nxt = []
        for m, w in enumerate(work):
            at = k - low
            pivot_row = w[at : at + 1, :]
            d = pivot_row[:, k : k + 1]
            root = lax.rsqrt(d)
            scaled = pivot_row * root
            done[m].append(scaled[:, size:])
            if k + 1 < size:
                column = w[:, k : k + 1] * root
                if at == 7:
                    nxt.append(w[8:] - column[8:] * scaled)
                else:
                    nxt.append(w - column * scaled)
        work = nxt
    return [jnp.concatenate(d, axis=0) for d in done]


def basis_kernel(
    own, place, row_terms, col_terms, omega_ref, psi_ref, weight_ref, row_ref, col_ref, aug
):
    width = omega_ref.shape[2]
    height = omega_ref.shape[1]
    for k in range(own):
        scale = weight_ref[pl.ds(place[0] * own + k, 1), :]
        for p in range(height // LANES):
            span = slice(p * LANES, (p + 1) * LANES)
            tile = upright(scale[:, span])
            for half in range(width // LANES):
                lanes = slice(half * LANES, (half + 1) * LANES)
                row_ref[k, span, lanes] = tile * omega_ref[k, span, lanes]
                col_ref[k, span, lanes] = tile * psi_ref[k, span, lanes]
        for terms, out in ((row_terms, row_ref), (col_terms, col_ref)):
            part = terms.shape[2]
            for c in range(terms.shape[0]):
                span = slice(c * part, (c + 1) * part)
                out[k, span, :] += terms[c, k]
    rows = lax.broadcasted_iota(jnp.int32, (width, width), 0)
    cols = lax.broadcasted_iota(jnp.int32, (width, width), 1)
    eye = (rows == cols).astype(jnp.float32)
    sources = [(out, k) for k in range(own) for out in (row_ref, col_ref)]
    for m, (out, k) in enumerate(sources):
        aug[m, :, :width] = dot(out[k], out[k], ((0,), (0,)))
        aug[m, :, width:] = eye
    steps = width // BASE
    lane = lax.broadcasted_iota(jnp.int32, (BASE, width), 1)
    for s in range(steps):
        span = slice(s * BASE, (s + 1) * BASE)
        inverses = invert_base([aug[m, span, span] for m in range(len(sources))])
        for m in range(len(sources)):
            panel = dot(inverses[m], aug[m, span, :], ((1,), (0,)))
            aug[m, span, :] = panel
            if s + 1 < steps:
                rest = slice((s + 1) * BASE, width)
                update = dot(jnp.where(lane >= (s + 1) * BASE, panel[:, :width], 0.0), panel, ((0,), (0,)))
                aug[m, rest, :] = aug[m, rest, :] - update[(s + 1) * BASE :]
    for m, (out, k) in enumerate(sources):
        out[k] = dot(out[k], aug[m, :, width:], ((1,), (1,)))


def move_psi(psi, own, ratio, row, col, n_row, n_col):
    first = lax.rem(col, ratio) * (own * n_row)
    result = None
    home = col // ratio
    for shift in range(n_row):
        target = lax.rem(home + shift, n_row)
        piece = lax.dynamic_slice_in_dim(psi, first + target * own, own, 0)
        if shift:
            pairs = [
                ((c // ratio) * n_col + c, ((c // ratio + shift) % n_row) * n_col + c) for c in range(n_col)
            ]
            piece = lax.ppermute(piece, ("row", "col"), pairs)
        result = piece if result is None else jnp.where(row == target, piece, result)
    return result


def per_device(positions, modulus, self_weight, omega, psi, blocks, *, n_row, n_col):
    col_clusters, height, width = omega.shape
    row_clusters = psi.shape[0]
    zones = positions.shape[1] // col_clusters
    ratio = row_clusters // col_clusters
    own = col_clusters // n_row
    row = lax.axis_index("row")
    col = lax.axis_index("col")
    pairs = blocks.reshape(-1, 2)
    slots = pairs.shape[0]
    own_psi = move_psi(psi, own, ratio, row, col, n_row, n_col)

    points = jnp.concatenate([positions, modulus[None]], axis=0)
    meta = jnp.pad(pairs.astype(jnp.float32).reshape(1, -1), ((0, 7), (0, LANES - 2 * slots)))
    all_points, all_meta = remote_call(
        functools.partial(gather_kernel, (n_row, n_col, ratio)),
        [f32(n_col, 4, positions.shape[1]), f32(n_col + n_row, 8, LANES)],
        2 * n_col + n_row,
        2 * n_col + n_row,
        1,
        [points, meta],
    )
    metas = all_meta[:, 0, : 2 * slots].astype(jnp.int32).reshape(n_col + n_row, slots, 2)
    row_ids = metas[:n_col, :, 0].reshape(-1)
    col_ids = metas[n_col:, :, 1].reshape(-1)

    def table(lefts, rights, base, extra):
        at = jnp.where(lefts >= 0, lefts + base, -1)
        return jnp.stack([at, rights, jnp.broadcast_to(extra, at.shape)], axis=-1)

    row_base = (jnp.arange(n_row * slots, dtype=jnp.int32) // slots) * row_clusters
    row_table = table(metas[n_col:, :, 0].reshape(-1), col_ids, row_base, row)
    col_table = table(pairs[:, 0], pairs[:, 1], row * row_clusters, row)

    def left_map(n, ids):
        at = jnp.maximum(ids[n, 0], 0)
        return (at // col_clusters, 0, at % col_clusters)

    def term_call(kernel, count, rows, clusters_map, scratch, name):
        return pl.pallas_call(
            kernel,
            out_shape=f32(count, rows, width),
            grid_spec=pltpu.PrefetchScalarGridSpec(
                num_scalar_prefetch=1,
                grid=(count,),
                in_specs=[
                    pl.BlockSpec((1, 4, zones), left_map),
                    pl.BlockSpec((4, zones), lambda n, ids: (0, jnp.maximum(ids[n, 1], 0))),
                    pl.BlockSpec((1, height, width), clusters_map),
                ],
                out_specs=pl.BlockSpec((1, rows, width), lambda n, ids: (n, 0, 0)),
                scratch_shapes=scratch,
            ),
            cost_estimate=pl.CostEstimate(
                flops=12 * count * rows * height * width, bytes_accessed=8 * count * height * width, transcendentals=0
            ),
            name=name,
        )

    row_terms = term_call(
        row_terms_kernel,
        n_row * slots,
        height // n_row,
        lambda n, ids: (jnp.maximum(ids[n, 1], 0), 0, 0),
        [pltpu.VMEM((4, zones, zones), jnp.float32)],
        "row_terms",
    )(row_table, all_points, points, omega)
    col_terms = term_call(
        col_terms_kernel,
        slots,
        height,
        lambda n, ids: (lax.rem(jnp.maximum(ids[n, 0], 0), row_clusters), 0, 0),
        [],
        "col_terms",
    )(col_table, all_points, points, psi)

    sizes = (n_row, n_col, ratio, own)
    row_part = height // n_col
    col_part = height // n_row
    got_rows, got_cols = remote_call(
        functools.partial(spread_kernel, sizes),
        [f32(n_col, slots, row_part, width), f32(n_row, slots, col_part, width)],
        n_col + n_row,
        n_col + n_row,
        2,
        [row_terms.reshape(n_row, slots, height // n_row, width), col_terms],
    )
    row_chunks, col_chunks = sum_terms(row_ids, col_ids, got_rows, got_cols, row_clusters, col_clusters)
    full_rows, full_cols = remote_call(
        functools.partial(collect_kernel, sizes),
        [f32(n_col, own, row_part, width), f32(n_row, own, col_part, width)],
        n_col + n_row,
        n_col + n_row,
        3,
        [row_chunks, col_chunks],
    )

    def whole(shape):
        return pl.BlockSpec(shape, lambda n, _: (0,) * len(shape), pipeline_mode=pl.Buffered(1))

    row_basis, col_basis = pl.pallas_call(
        functools.partial(basis_kernel, own),
        out_shape=[f32(own, height, width), f32(own, height, width)],
        grid_spec=pltpu.PrefetchScalarGridSpec(
            num_scalar_prefetch=1,
            grid=(1,),
            in_specs=[
                whole(full_rows.shape),
                whole(full_cols.shape),
                pl.BlockSpec((own, height, width), lambda n, at: (at[0], 0, 0), pipeline_mode=pl.Buffered(1)),
                whole(own_psi.shape),
                whole(self_weight.shape),
            ],
            out_specs=[whole(own_psi.shape), whole(own_psi.shape)],
            scratch_shapes=[pltpu.VMEM((2 * own, width, 2 * width), jnp.float32)],
        ),
        name="basis",
    )(row.astype(jnp.int32)[None], full_rows, full_cols, omega, own_psi, self_weight)
    return tuple(
        remote_call(
            functools.partial(deliver_kernel, sizes),
            [f32(row_clusters, row_part, width), f32(col_clusters, col_part, width)],
            n_col + n_row,
            n_col + n_row,
            4,
            [row_basis, col_basis],
        )
    )


def solution(mesh):
    placed = (
        P(None, "col"),
        P("col"),
        P("col", None),
        P("col", None, None),
        P("row", None, None),
        P("row", "col", None, None),
    )
    return jax.shard_map(
        functools.partial(per_device, n_row=mesh.shape["row"], n_col=mesh.shape["col"]),
        mesh=mesh,
        in_specs=placed,
        out_specs=(P("row", "col", None), P("col", "row", None)),
        check_vma=False,
    )
```

```python
import functools
import math

import jax
import jax.numpy as jnp
from jax import lax
from jax.experimental import pallas as pl
from jax.experimental.pallas import tpu as pltpu
from jax.sharding import PartitionSpec as P

COUPLE = 0.25
ROOT_TWO = 1.4142135623730951
HIGH = lax.Precision.HIGHEST
BASE = 64
GROUP = 4
LANES = 128
MESH = pl.DeviceIdType.MESH
ANY = pl.BlockSpec(memory_space=pl.ANY)


def exchange(outgoing, incoming, barrier, send_sem, recv_sem, local_sem):
    row = lax.axis_index("row")
    col = lax.axis_index("col")
    remote_out = jnp.int32(0)
    for _, device, _, cond in incoming:
        here = jnp.logical_and(device[0] == row, device[1] == col)

        @pl.when(jnp.logical_and(cond, jnp.logical_not(here)))
        def _():
            pl.semaphore_signal(barrier, inc=1, device_id=device, device_id_type=MESH)

    for _, _, device, _, cond in outgoing:
        here = jnp.logical_and(device[0] == row, device[1] == col)
        remote_out = remote_out + jnp.logical_and(cond, jnp.logical_not(here)).astype(jnp.int32)
    pl.semaphore_wait(barrier, remote_out)

    def each_out(action):
        for number, (src, dst, device, slot, cond) in enumerate(outgoing):
            here = jnp.logical_and(device[0] == row, device[1] == col)
            remote = pltpu.make_async_remote_copy(
                src_ref=src,
                dst_ref=dst,
                send_sem=send_sem.at[number],
                recv_sem=recv_sem.at[slot],
                device_id=device,
                device_id_type=MESH,
            )
            local = pltpu.make_async_copy(src, dst, local_sem.at[number])

            @pl.when(jnp.logical_and(cond, jnp.logical_not(here)))
            def _():
                remote.start() if action == "start" else remote.wait_send()

            @pl.when(jnp.logical_and(cond, here))
            def _():
                local.start() if action == "start" else local.wait()

    each_out("start")
    for dst, device, slot, cond in incoming:
        here = jnp.logical_and(device[0] == row, device[1] == col)

        @pl.when(jnp.logical_and(cond, jnp.logical_not(here)))
        def _():
            pltpu.make_async_remote_copy(
                src_ref=dst,
                dst_ref=dst,
                send_sem=send_sem.at[0],
                recv_sem=recv_sem.at[slot],
                device_id=device,
                device_id_type=MESH,
            ).wait_recv()

    each_out("wait")


def remote_call(body, out_shapes, sems_out, sems_in, ident, operands):
    return pl.pallas_call(
        body,
        out_shape=out_shapes,
        in_specs=[ANY] * len(operands),
        out_specs=[ANY] * len(out_shapes),
        scratch_shapes=[
            pltpu.SemaphoreType.DMA((sems_out,)),
            pltpu.SemaphoreType.DMA((sems_in,)),
            pltpu.SemaphoreType.DMA((sems_out,)),
        ],
        compiler_params=pltpu.CompilerParams(collective_id=ident, has_side_effects=True),
        name="exchange_%d" % ident,
    )(*operands)


def f32(*shape):
    return jax.ShapeDtypeStruct(shape, jnp.float32)


def gather_kernel(sizes, points_ref, meta_ref, out_points, out_meta, send_sem, recv_sem, local_sem):
    n_row, n_col, ratio = sizes
    row = lax.axis_index("row")
    col = lax.axis_index("col")
    yes = jnp.bool_(True)
    outgoing, incoming = [], []
    for c in range(n_col):
        outgoing.append((points_ref, out_points.at[col], (row, c), col, yes))
        incoming.append((out_points.at[c], (row, c), c, yes))
    for q in range(n_col):
        outgoing.append(
            (meta_ref, out_meta.at[col], (q // ratio, row * ratio + q % ratio), n_col + col, yes)
        )
        incoming.append((out_meta.at[q], (col // ratio, q), n_col + q, yes))
    for p in range(n_row):
        outgoing.append((meta_ref, out_meta.at[n_col + row], (p, col), 2 * n_col + row, yes))
        incoming.append((out_meta.at[n_col + p], (p, col), 2 * n_col + p, yes))
    exchange(outgoing, incoming, pltpu.get_barrier_semaphore(), send_sem, recv_sem, local_sem)


def spread_kernel(sizes, row_terms, col_terms, out_rows, out_cols, send_sem, recv_sem, local_sem):
    n_row, n_col, ratio, own = sizes
    row = lax.axis_index("row")
    col = lax.axis_index("col")
    yes = jnp.bool_(True)
    row_part = out_rows.shape[2]
    col_part = out_cols.shape[2]
    outgoing, incoming = [], []
    for c in range(n_col):
        x = c % ratio
        outgoing.append(
            (
                row_terms.at[c // ratio, :, x * row_part : (x + 1) * row_part],
                out_rows.at[col],
                (row, c),
                col,
                yes,
            )
        )
        incoming.append((out_rows.at[c], (row, c), c, yes))
    for p in range(n_row):
        outgoing.append(
            (col_terms.at[:, p * col_part : (p + 1) * col_part], out_cols.at[row], (p, col), n_col + row, yes)
        )
        incoming.append((out_cols.at[p], (p, col), n_col + p, yes))
    exchange(outgoing, incoming, pltpu.get_barrier_semaphore(), send_sem, recv_sem, local_sem)


def collect_kernel(sizes, rows, cols, out_rows, out_cols, send_sem, recv_sem, local_sem):
    n_row, n_col, ratio, own = sizes
    row = lax.axis_index("row")
    col = lax.axis_index("col")
    yes = jnp.bool_(True)
    group = col // ratio
    mine = row * ratio + lax.rem(col, ratio)
    outgoing, incoming = [], []
    for q in range(n_col):
        device = (q // ratio, group * ratio + q % ratio)
        start = (q % ratio) * (own * n_row) + (q // ratio) * own
        outgoing.append((rows.at[pl.ds(start, own)], out_rows.at[mine], device, mine, yes))
        incoming.append((out_rows.at[q], device, q, yes))
    for p in range(n_row):
        outgoing.append((cols.at[pl.ds(p * own, own)], out_cols.at[row], (p, col), n_col + row, yes))
        incoming.append((out_cols.at[p], (p, col), n_col + p, yes))
    exchange(outgoing, incoming, pltpu.get_barrier_semaphore(), send_sem, recv_sem, local_sem)


def deliver_kernel(sizes, rows, cols, out_rows, out_cols, send_sem, recv_sem, local_sem):
    n_row, n_col, ratio, own = sizes
    row = lax.axis_index("row")
    col = lax.axis_index("col")
    yes = jnp.bool_(True)
    row_part = rows.shape[1] // n_col
    col_part = cols.shape[1] // n_row
    outgoing, incoming = [], []
    mine = row * ratio + lax.rem(col, ratio)
    place = lax.rem(col, ratio) * (own * n_row) + row * own
    for c in range(n_col):
        outgoing.append(
            (
                rows.at[:, c * row_part : (c + 1) * row_part],
                out_rows.at[pl.ds(place, own)],
                (col // ratio, c),
                mine,
                yes,
            )
        )
        start = (c % ratio) * (own * n_row) + (c // ratio) * own
        incoming.append((out_rows.at[pl.ds(start, own)], (c // ratio, row * ratio + c % ratio), c, yes))
    for p in range(n_row):
        outgoing.append(
            (
                cols.at[:, p * col_part : (p + 1) * col_part],
                out_cols.at[pl.ds(row * own, own)],
                (p, col),
                n_col + row,
                yes,
            )
        )
        incoming.append((out_cols.at[pl.ds(p * own, own)], (p, col), n_col + p, yes))
    exchange(outgoing, incoming, pltpu.get_barrier_semaphore(), send_sem, recv_sem, local_sem)


def dot(a, b, contract):
    return lax.dot_general(
        a, b, (contract, ((), ())), precision=HIGH, preferred_element_type=jnp.float32
    )


def upright(line):
    size = line.shape[1]
    return jnp.transpose(jnp.broadcast_to(line, (size, size)))


def shape_of(left, right_ref):
    offs = [left[n] - right_ref[n : n + 1, :] for n in range(3)]
    spread = (offs[0] * offs[0] + offs[1] * offs[1] + offs[2] * offs[2]) + 1.0
    inverse = lax.rsqrt(spread)
    nx, ny, nz = [o * inverse for o in offs]
    weight = COUPLE * inverse * inverse * inverse * left[3] * right_ref[3:4, :]
    u = [nx * nx, ny * ny, nz * nz, ROOT_TWO * ny * nz, ROOT_TWO * nx * nz, ROOT_TWO * nx * ny]
    return u, weight


def row_terms_kernel(ids, left_ref, right_ref, omega_ref, out_ref, held):
    n = pl.program_id(0)
    live = ids[n, 0] >= 0
    slab = ids[n, 2]
    zones = right_ref.shape[1]
    rows = out_ref.shape[1]
    step = math.gcd(zones, rows)
    per = zones // step

    @pl.when(jnp.logical_not(live))
    def _():
        out_ref[...] = jnp.zeros_like(out_ref)

    @pl.when(live)
    def _():
        for m in range(4):
            held[m] = upright(left_ref[0, m : m + 1, :])
        for g in range(rows // step):
            which = slab * (rows // step) + g
            p = which // per
            start = pl.multiple_of((which % per) * step, step)
            u, weight = shape_of([held[m, pl.ds(start, step), :] for m in range(4)], right_ref)
            mine = u[5]
            for k in range(5):
                mine = jnp.where(p == k, u[k], mine)
            trace = (p < 3).astype(jnp.float32)
            parts = []
            for q in range(6):
                val = trace * u[q] - 5.0 * mine * u[q] + (p == q).astype(jnp.float32)
                if q < 3:
                    val = val + mine
                parts.append(weight * val)
            strip = jnp.concatenate(parts, axis=1)
            out_ref[0, g * step : (g + 1) * step, :] = dot(strip, omega_ref[0], ((1,), (0,)))


def col_terms_kernel(ids, left_ref, right_ref, psi_ref, out_ref):
    n = pl.program_id(0)
    live = ids[n, 0] >= 0
    zones = right_ref.shape[1]

    @pl.when(jnp.logical_not(live))
    def _():
        out_ref[...] = jnp.zeros_like(out_ref)

    @pl.when(live)
    def _():
        left = [upright(right_ref[m : m + 1, :]) for m in range(4)]
        u, weight = shape_of(left, left_ref.at[0])
        for p in range(6):
            parts = []
            for q in range(6):
                val = -5.0 * u[p] * u[q]
                if q < 3:
                    val = val + u[p]
                if p < 3:
                    val = val + u[q]
                if p == q:
                    val = val + 1.0
                parts.append(weight * val)
            strip = jnp.concatenate(parts, axis=1)
            out_ref[0, p * zones : (p + 1) * zones, :] = dot(strip, psi_ref[0], ((1,), (0,)))


def add_kernel(row_ids, col_ids, rows_ref, cols_ref, out_rows, out_cols):
    for ids, terms_ref, out_ref in ((row_ids, rows_ref, out_rows), (col_ids, cols_ref, out_cols)):
        out_ref[...] = jnp.zeros_like(out_ref)
        slots = terms_ref.shape[1]

        @pl.loop(0, terms_ref.shape[0] * slots)
        def _(n):
            target = ids[n]

            @pl.when(target >= 0)
            def _():
                out_ref[target] += terms_ref[n // slots, n % slots]


def sum_terms(row_ids, col_ids, rows, cols, row_clusters, col_clusters):
    whole = pl.BlockSpec(memory_space=pltpu.VMEM)
    table = pl.BlockSpec(memory_space=pltpu.SMEM)
    return pl.pallas_call(
        add_kernel,
        out_shape=[f32(row_clusters, *rows.shape[2:]), f32(col_clusters, *cols.shape[2:])],
        in_specs=[table, table, whole, whole],
        out_specs=[whole, whole],
        name="sum_terms",
    )(row_ids, col_ids, rows, cols)


def invert_base(blocks):
    size = blocks[0].shape[0]
    wide = (8, 2 * size)
    rows = lax.broadcasted_iota(jnp.int32, (size, size), 0)
    cols = lax.broadcasted_iota(jnp.int32, (size, size), 1)
    eye = (rows == cols).astype(jnp.float32)
    sub = lax.broadcasted_iota(jnp.int32, wide, 0)
    work = []
    for b in blocks:
        both = jnp.concatenate([b, eye], axis=1)
        work.append([both[8 * t : 8 * t + 8] for t in range(size // 8)])
    done = [[] for _ in blocks]
    for k in range(0, size, GROUP):
        first = k // 8
        at = k % 8
        for m, tiles in enumerate(work):
            line = [jnp.broadcast_to(tiles[first][at + a : at + a + 1, :], wide) for a in range(GROUP)]
            side = [
                [jnp.broadcast_to(tiles[t][:, k + a : k + a + 1], wide) for t in range(first, size // 8)]
                for a in range(GROUP)
            ]
            small = [
                [jnp.broadcast_to(line[a][:, k + c : k + c + 1], wide) for c in range(a + 1)] for a in range(GROUP)
            ]
            for c in range(GROUP):
                root = lax.rsqrt(small[c][c])
                line[c] = line[c] * root
                side[c] = [v * root for v in side[c]]
                factor = [small[a][c] * root for a in range(c + 1, GROUP)]
                for a in range(c + 1, GROUP):
                    f = factor[a - c - 1]
                    line[a] = line[a] - f * line[c]
                    side[a] = [v - f * w for v, w in zip(side[a], side[c])]
                    for e in range(c + 1, a + 1):
                        small[a][e] = small[a][e] - f * factor[e - c - 1]
            if at == 0:
                done[m].append(line[0])
            for a in range(GROUP):
                done[m][first] = jnp.where(sub == at + a, line[a], done[m][first])
            stay = first + (at + GROUP == 8)
            for t in range(stay, size // 8):
                for a in range(GROUP):
                    tiles[t] = tiles[t] - side[a][t - first] * line[a]
    return [jnp.concatenate(d, axis=0)[:, size:] for d in done]


def basis_kernel(
    own, place, row_terms, col_terms, omega_ref, psi_ref, weight_ref, row_ref, col_ref, aug
):
    width = omega_ref.shape[2]
    height = omega_ref.shape[1]
    for k in range(own):
        scale = weight_ref[pl.ds(place[0] * own + k, 1), :]
        for p in range(height // LANES):
            span = slice(p * LANES, (p + 1) * LANES)
            tile = upright(scale[:, span])
            for half in range(width // LANES):
                lanes = slice(half * LANES, (half + 1) * LANES)
                row_ref[k, span, lanes] = tile * omega_ref[k, span, lanes]
                col_ref[k, span, lanes] = tile * psi_ref[k, span, lanes]
        for terms, out in ((row_terms, row_ref), (col_terms, col_ref)):
            part = terms.shape[2]
            for c in range(terms.shape[0]):
                span = slice(c * part, (c + 1) * part)
                out[k, span, :] += terms[c, k]
    rows = lax.broadcasted_iota(jnp.int32, (width, width), 0)
    cols = lax.broadcasted_iota(jnp.int32, (width, width), 1)
    eye = (rows == cols).astype(jnp.float32)
    sources = [(out, k) for k in range(own) for out in (row_ref, col_ref)]
    for m, (out, k) in enumerate(sources):
        aug[m, :, :width] = dot(out[k], out[k], ((0,), (0,)))
        aug[m, :, width:] = eye
    steps = width // BASE
    lane = lax.broadcasted_iota(jnp.int32, (BASE, width), 1)
    for s in range(steps):
        span = slice(s * BASE, (s + 1) * BASE)
        inverses = invert_base([aug[m, span, span] for m in range(len(sources))])
        for m in range(len(sources)):
            panel = dot(inverses[m], aug[m, span, :], ((1,), (0,)))
            aug[m, span, :] = panel
            if s + 1 < steps:
                rest = slice((s + 1) * BASE, width)
                update = dot(jnp.where(lane >= (s + 1) * BASE, panel[:, :width], 0.0), panel, ((0,), (0,)))
                aug[m, rest, :] = aug[m, rest, :] - update[(s + 1) * BASE :]
    for m, (out, k) in enumerate(sources):
        out[k] = dot(out[k], aug[m, :, width:], ((1,), (1,)))


def move_psi(psi, own, ratio, row, col, n_row, n_col):
    first = lax.rem(col, ratio) * (own * n_row)
    result = None
    home = col // ratio
    for shift in range(n_row):
        target = lax.rem(home + shift, n_row)
        piece = lax.dynamic_slice_in_dim(psi, first + target * own, own, 0)
        if shift:
            pairs = [
                ((c // ratio) * n_col + c, ((c // ratio + shift) % n_row) * n_col + c) for c in range(n_col)
            ]
            piece = lax.ppermute(piece, ("row", "col"), pairs)
        result = piece if result is None else jnp.where(row == target, piece, result)
    return result


def per_device(positions, modulus, self_weight, omega, psi, blocks, *, n_row, n_col):
    col_clusters, height, width = omega.shape
    row_clusters = psi.shape[0]
    zones = positions.shape[1] // col_clusters
    ratio = row_clusters // col_clusters
    own = col_clusters // n_row
    row = lax.axis_index("row")
    col = lax.axis_index("col")
    pairs = blocks.reshape(-1, 2)
    slots = pairs.shape[0]

    points = jnp.concatenate([positions, modulus[None]], axis=0)
    meta = jnp.pad(pairs.astype(jnp.float32).reshape(1, -1), ((0, 7), (0, LANES - 2 * slots)))
    all_points, all_meta = remote_call(
        functools.partial(gather_kernel, (n_row, n_col, ratio)),
        [f32(n_col, 4, positions.shape[1]), f32(n_col + n_row, 8, LANES)],
        2 * n_col + n_row,
        2 * n_col + n_row,
        1,
        [points, meta],
    )
    all_points, all_meta, late_psi = lax.optimization_barrier((all_points, all_meta, psi))
    own_psi = move_psi(late_psi, own, ratio, row, col, n_row, n_col)
    metas = all_meta[:, 0, : 2 * slots].astype(jnp.int32).reshape(n_col + n_row, slots, 2)
    row_ids = metas[:n_col, :, 0].reshape(-1)
    col_ids = metas[n_col:, :, 1].reshape(-1)

    def table(lefts, rights, base, extra):
        at = jnp.where(lefts >= 0, lefts + base, -1)
        return jnp.stack([at, rights, jnp.broadcast_to(extra, at.shape)], axis=-1)

    row_base = (jnp.arange(n_row * slots, dtype=jnp.int32) // slots) * row_clusters
    row_table = table(metas[n_col:, :, 0].reshape(-1), col_ids, row_base, row)
    col_table = table(pairs[:, 0], pairs[:, 1], row * row_clusters, row)

    def left_map(n, ids):
        at = jnp.maximum(ids[n, 0], 0)
        return (at // col_clusters, 0, at % col_clusters)

    def term_call(kernel, count, rows, clusters_map, scratch, name):
        return pl.pallas_call(
            kernel,
            out_shape=f32(count, rows, width),
            grid_spec=pltpu.PrefetchScalarGridSpec(
                num_scalar_prefetch=1,
                grid=(count,),
                in_specs=[
                    pl.BlockSpec((1, 4, zones), left_map),
                    pl.BlockSpec((4, zones), lambda n, ids: (0, jnp.maximum(ids[n, 1], 0))),
                    pl.BlockSpec((1, height, width), clusters_map),
                ],
                out_specs=pl.BlockSpec((1, rows, width), lambda n, ids: (n, 0, 0)),
                scratch_shapes=scratch,
            ),
            cost_estimate=pl.CostEstimate(
                flops=12 * count * rows * height * width, bytes_accessed=8 * count * height * width, transcendentals=0
            ),
            name=name,
        )

    row_terms = term_call(
        row_terms_kernel,
        n_row * slots,
        height // n_row,
        lambda n, ids: (jnp.maximum(ids[n, 1], 0), 0, 0),
        [pltpu.VMEM((4, zones, zones), jnp.float32)],
        "row_terms",
    )(row_table, all_points, points, omega)
    col_terms = term_call(
        col_terms_kernel,
        slots,
        height,
        lambda n, ids: (lax.rem(jnp.maximum(ids[n, 0], 0), row_clusters), 0, 0),
        [],
        "col_terms",
    )(col_table, all_points, points, psi)

    sizes = (n_row, n_col, ratio, own)
    row_part = height // n_col
    col_part = height // n_row
    got_rows, got_cols = remote_call(
        functools.partial(spread_kernel, sizes),
        [f32(n_col, slots, row_part, width), f32(n_row, slots, col_part, width)],
        n_col + n_row,
        n_col + n_row,
        2,
        [row_terms.reshape(n_row, slots, height // n_row, width), col_terms],
    )
    row_chunks, col_chunks = sum_terms(row_ids, col_ids, got_rows, got_cols, row_clusters, col_clusters)
    full_rows, full_cols = remote_call(
        functools.partial(collect_kernel, sizes),
        [f32(n_col, own, row_part, width), f32(n_row, own, col_part, width)],
        n_col + n_row,
        n_col + n_row,
        3,
        [row_chunks, col_chunks],
    )

    def whole(shape):
        return pl.BlockSpec(shape, lambda n, _: (0,) * len(shape), pipeline_mode=pl.Buffered(1))

    row_basis, col_basis = pl.pallas_call(
        functools.partial(basis_kernel, own),
        out_shape=[f32(own, height, width), f32(own, height, width)],
        grid_spec=pltpu.PrefetchScalarGridSpec(
            num_scalar_prefetch=1,
            grid=(1,),
            in_specs=[
                whole(full_rows.shape),
                whole(full_cols.shape),
                pl.BlockSpec((own, height, width), lambda n, at: (at[0], 0, 0), pipeline_mode=pl.Buffered(1)),
                whole(own_psi.shape),
                whole(self_weight.shape),
            ],
            out_specs=[whole(own_psi.shape), whole(own_psi.shape)],
            scratch_shapes=[pltpu.VMEM((2 * own, width, 2 * width), jnp.float32)],
        ),
        name="basis",
    )(row.astype(jnp.int32)[None], full_rows, full_cols, omega, own_psi, self_weight)
    return tuple(
        remote_call(
            functools.partial(deliver_kernel, sizes),
            [f32(row_clusters, row_part, width), f32(col_clusters, col_part, width)],
            n_col + n_row,
            n_col + n_row,
            4,
            [row_basis, col_basis],
        )
    )


def solution(mesh):
    placed = (
        P(None, "col"),
        P("col"),
        P("col", None),
        P("col", None, None),
        P("row", None, None),
        P("row", "col", None, None),
    )
    return jax.shard_map(
        functools.partial(per_device, n_row=mesh.shape["row"], n_col=mesh.shape["col"]),
        mesh=mesh,
        in_specs=placed,
        out_specs=(P("row", "col", None), P("col", "row", None)),
        check_vma=False,
    )
```

```python
import functools
import math

import jax
import jax.numpy as jnp
from jax import lax
from jax.experimental import pallas as pl
from jax.experimental.pallas import tpu as pltpu
from jax.sharding import PartitionSpec as P

COUPLE = 0.25
ROOT_TWO = 1.4142135623730951
HIGH = lax.Precision.HIGHEST
BASE = 64
GROUP = 4
LANES = 128
MESH = pl.DeviceIdType.MESH
ANY = pl.BlockSpec(memory_space=pl.ANY)


def exchange(outgoing, incoming, barrier, send_sem, recv_sem, local_sem):
    row = lax.axis_index("row")
    col = lax.axis_index("col")
    remote_out = jnp.int32(0)
    for _, device, _, cond in incoming:
        here = jnp.logical_and(device[0] == row, device[1] == col)

        @pl.when(jnp.logical_and(cond, jnp.logical_not(here)))
        def _():
            pl.semaphore_signal(barrier, inc=1, device_id=device, device_id_type=MESH)

    for _, _, device, _, cond in outgoing:
        here = jnp.logical_and(device[0] == row, device[1] == col)
        remote_out = remote_out + jnp.logical_and(cond, jnp.logical_not(here)).astype(jnp.int32)
    pl.semaphore_wait(barrier, remote_out)

    def each_out(action):
        for number, (src, dst, device, slot, cond) in enumerate(outgoing):
            here = jnp.logical_and(device[0] == row, device[1] == col)
            remote = pltpu.make_async_remote_copy(
                src_ref=src,
                dst_ref=dst,
                send_sem=send_sem.at[number],
                recv_sem=recv_sem.at[slot],
                device_id=device,
                device_id_type=MESH,
            )
            local = pltpu.make_async_copy(src, dst, local_sem.at[number])

            @pl.when(jnp.logical_and(cond, jnp.logical_not(here)))
            def _():
                remote.start() if action == "start" else remote.wait_send()

            @pl.when(jnp.logical_and(cond, here))
            def _():
                local.start() if action == "start" else local.wait()

    each_out("start")
    for dst, device, slot, cond in incoming:
        here = jnp.logical_and(device[0] == row, device[1] == col)

        @pl.when(jnp.logical_and(cond, jnp.logical_not(here)))
        def _():
            pltpu.make_async_remote_copy(
                src_ref=dst,
                dst_ref=dst,
                send_sem=send_sem.at[0],
                recv_sem=recv_sem.at[slot],
                device_id=device,
                device_id_type=MESH,
            ).wait_recv()

    each_out("wait")


def remote_call(body, out_shapes, sems_out, sems_in, ident, operands):
    return pl.pallas_call(
        body,
        out_shape=out_shapes,
        in_specs=[ANY] * len(operands),
        out_specs=[ANY] * len(out_shapes),
        scratch_shapes=[
            pltpu.SemaphoreType.DMA((sems_out,)),
            pltpu.SemaphoreType.DMA((sems_in,)),
            pltpu.SemaphoreType.DMA((sems_out,)),
        ],
        compiler_params=pltpu.CompilerParams(collective_id=ident, has_side_effects=True),
        name="exchange_%d" % ident,
    )(*operands)


def f32(*shape):
    return jax.ShapeDtypeStruct(shape, jnp.float32)


def gather_kernel(sizes, points_ref, meta_ref, out_points, out_meta, send_sem, recv_sem, local_sem):
    n_row, n_col, ratio = sizes
    row = lax.axis_index("row")
    col = lax.axis_index("col")
    yes = jnp.bool_(True)
    outgoing, incoming = [], []
    for c in range(n_col):
        outgoing.append((points_ref, out_points.at[col], (row, c), col, yes))
        incoming.append((out_points.at[c], (row, c), c, yes))
    for q in range(n_col):
        outgoing.append(
            (meta_ref, out_meta.at[col], (q // ratio, row * ratio + q % ratio), n_col + col, yes)
        )
        incoming.append((out_meta.at[q], (col // ratio, q), n_col + q, yes))
    for p in range(n_row):
        outgoing.append((meta_ref, out_meta.at[n_col + row], (p, col), 2 * n_col + row, yes))
        incoming.append((out_meta.at[n_col + p], (p, col), 2 * n_col + p, yes))
    exchange(outgoing, incoming, pltpu.get_barrier_semaphore(), send_sem, recv_sem, local_sem)


def spread_kernel(sizes, row_terms, col_terms, out_rows, out_cols, send_sem, recv_sem, local_sem):
    n_row, n_col, ratio, own = sizes
    row = lax.axis_index("row")
    col = lax.axis_index("col")
    yes = jnp.bool_(True)
    row_part = out_rows.shape[2]
    col_part = out_cols.shape[2]
    outgoing, incoming = [], []
    for c in range(n_col):
        x = c % ratio
        outgoing.append(
            (
                row_terms.at[c // ratio, :, x * row_part : (x + 1) * row_part],
                out_rows.at[col],
                (row, c),
                col,
                yes,
            )
        )
        incoming.append((out_rows.at[c], (row, c), c, yes))
    for p in range(n_row):
        outgoing.append(
            (col_terms.at[:, p * col_part : (p + 1) * col_part], out_cols.at[row], (p, col), n_col + row, yes)
        )
        incoming.append((out_cols.at[p], (p, col), n_col + p, yes))
    exchange(outgoing, incoming, pltpu.get_barrier_semaphore(), send_sem, recv_sem, local_sem)


def collect_kernel(sizes, rows, cols, out_rows, out_cols, send_sem, recv_sem, local_sem):
    n_row, n_col, ratio, own = sizes
    row = lax.axis_index("row")
    col = lax.axis_index("col")
    yes = jnp.bool_(True)
    group = col // ratio
    mine = row * ratio + lax.rem(col, ratio)
    outgoing, incoming = [], []
    for q in range(n_col):
        device = (q // ratio, group * ratio + q % ratio)
        start = (q % ratio) * (own * n_row) + (q // ratio) * own
        outgoing.append((rows.at[pl.ds(start, own)], out_rows.at[mine], device, mine, yes))
        incoming.append((out_rows.at[q], device, q, yes))
    for p in range(n_row):
        outgoing.append((cols.at[pl.ds(p * own, own)], out_cols.at[row], (p, col), n_col + row, yes))
        incoming.append((out_cols.at[p], (p, col), n_col + p, yes))
    exchange(outgoing, incoming, pltpu.get_barrier_semaphore(), send_sem, recv_sem, local_sem)


def deliver_kernel(sizes, rows, cols, out_rows, out_cols, send_sem, recv_sem, local_sem):
    n_row, n_col, ratio, own = sizes
    row = lax.axis_index("row")
    col = lax.axis_index("col")
    yes = jnp.bool_(True)
    row_part = rows.shape[1] // n_col
    col_part = cols.shape[1] // n_row
    outgoing, incoming = [], []
    mine = row * ratio + lax.rem(col, ratio)
    place = lax.rem(col, ratio) * (own * n_row) + row * own
    for c in range(n_col):
        outgoing.append(
            (
                rows.at[:, c * row_part : (c + 1) * row_part],
                out_rows.at[pl.ds(place, own)],
                (col // ratio, c),
                mine,
                yes,
            )
        )
        start = (c % ratio) * (own * n_row) + (c // ratio) * own
        incoming.append((out_rows.at[pl.ds(start, own)], (c // ratio, row * ratio + c % ratio), c, yes))
    for p in range(n_row):
        outgoing.append(
            (
                cols.at[:, p * col_part : (p + 1) * col_part],
                out_cols.at[pl.ds(row * own, own)],
                (p, col),
                n_col + row,
                yes,
            )
        )
        incoming.append((out_cols.at[pl.ds(p * own, own)], (p, col), n_col + p, yes))
    exchange(outgoing, incoming, pltpu.get_barrier_semaphore(), send_sem, recv_sem, local_sem)


def dot(a, b, contract):
    return lax.dot_general(
        a, b, (contract, ((), ())), precision=HIGH, preferred_element_type=jnp.float32
    )


def dot_split(a, b):
    a_high = a.astype(jnp.bfloat16)
    b_high = b.astype(jnp.bfloat16)
    a_low = (a - a_high.astype(jnp.float32)).astype(jnp.bfloat16)
    b_low = (b - b_high.astype(jnp.float32)).astype(jnp.bfloat16)
    total = jnp.dot(a_high, b_low, preferred_element_type=jnp.float32)
    total = total + jnp.dot(a_low, b_high, preferred_element_type=jnp.float32)
    return total + jnp.dot(a_high, b_high, preferred_element_type=jnp.float32)


def upright(line):
    size = line.shape[1]
    return jnp.transpose(jnp.broadcast_to(line, (size, size)))


def shape_of(left, right_ref):
    offs = [left[n] - right_ref[n : n + 1, :] for n in range(3)]
    spread = (offs[0] * offs[0] + offs[1] * offs[1] + offs[2] * offs[2]) + 1.0
    inverse = lax.rsqrt(spread)
    nx, ny, nz = [o * inverse for o in offs]
    weight = COUPLE * inverse * inverse * inverse * left[3] * right_ref[3:4, :]
    u = [nx * nx, ny * ny, nz * nz, ROOT_TWO * ny * nz, ROOT_TWO * nx * nz, ROOT_TWO * nx * ny]
    return u, weight


def row_terms_kernel(ids, left_ref, right_ref, omega_ref, out_ref, held):
    n = pl.program_id(0)
    live = ids[n, 0] >= 0
    slab = ids[n, 2]
    zones = right_ref.shape[1]
    rows = out_ref.shape[1]
    step = math.gcd(zones, rows)
    per = zones // step

    @pl.when(jnp.logical_not(live))
    def _():
        out_ref[...] = jnp.zeros_like(out_ref)

    @pl.when(live)
    def _():
        for m in range(4):
            held[m] = upright(left_ref[0, m : m + 1, :])
        for g in range(rows // step):
            which = slab * (rows // step) + g
            p = which // per
            start = pl.multiple_of((which % per) * step, step)
            u, weight = shape_of([held[m, pl.ds(start, step), :] for m in range(4)], right_ref)
            mine = u[5]
            for k in range(5):
                mine = jnp.where(p == k, u[k], mine)
            trace = (p < 3).astype(jnp.float32)
            parts = []
            for q in range(6):
                val = trace * u[q] - 5.0 * mine * u[q] + (p == q).astype(jnp.float32)
                if q < 3:
                    val = val + mine
                parts.append(weight * val)
            strip = jnp.concatenate(parts, axis=1)
            out_ref[0, g * step : (g + 1) * step, :] = dot_split(strip, omega_ref[0])


def col_terms_kernel(ids, left_ref, right_ref, psi_ref, out_ref):
    n = pl.program_id(0)
    live = ids[n, 0] >= 0
    zones = right_ref.shape[1]

    @pl.when(jnp.logical_not(live))
    def _():
        out_ref[...] = jnp.zeros_like(out_ref)

    @pl.when(live)
    def _():
        left = [upright(right_ref[m : m + 1, :]) for m in range(4)]
        u, weight = shape_of(left, left_ref.at[0])
        for p in range(6):
            parts = []
            for q in range(6):
                val = -5.0 * u[p] * u[q]
                if q < 3:
                    val = val + u[p]
                if p < 3:
                    val = val + u[q]
                if p == q:
                    val = val + 1.0
                parts.append(weight * val)
            strip = jnp.concatenate(parts, axis=1)
            out_ref[0, p * zones : (p + 1) * zones, :] = dot_split(strip, psi_ref[0])


def add_kernel(row_ids, col_ids, rows_ref, cols_ref, out_rows, out_cols):
    for ids, terms_ref, out_ref in ((row_ids, rows_ref, out_rows), (col_ids, cols_ref, out_cols)):
        out_ref[...] = jnp.zeros_like(out_ref)
        slots = terms_ref.shape[1]

        @pl.loop(0, terms_ref.shape[0] * slots)
        def _(n):
            target = ids[n]

            @pl.when(target >= 0)
            def _():
                out_ref[target] += terms_ref[n // slots, n % slots]


def sum_terms(row_ids, col_ids, rows, cols, row_clusters, col_clusters):
    whole = pl.BlockSpec(memory_space=pltpu.VMEM)
    table = pl.BlockSpec(memory_space=pltpu.SMEM)
    return pl.pallas_call(
        add_kernel,
        out_shape=[f32(row_clusters, *rows.shape[2:]), f32(col_clusters, *cols.shape[2:])],
        in_specs=[table, table, whole, whole],
        out_specs=[whole, whole],
        name="sum_terms",
    )(row_ids, col_ids, rows, cols)


def invert_base(blocks):
    size = blocks[0].shape[0]
    wide = (8, 2 * size)
    rows = lax.broadcasted_iota(jnp.int32, (size, size), 0)
    cols = lax.broadcasted_iota(jnp.int32, (size, size), 1)
    eye = (rows == cols).astype(jnp.float32)
    sub = lax.broadcasted_iota(jnp.int32, wide, 0)
    work = []
    for b in blocks:
        both = jnp.concatenate([b, eye], axis=1)
        work.append([both[8 * t : 8 * t + 8] for t in range(size // 8)])
    done = [[] for _ in blocks]
    for k in range(0, size, GROUP):
        first = k // 8
        at = k % 8
        for m, tiles in enumerate(work):
            line = [jnp.broadcast_to(tiles[first][at + a : at + a + 1, :], wide) for a in range(GROUP)]
            side = [
                [jnp.broadcast_to(tiles[t][:, k + a : k + a + 1], wide) for t in range(first, size // 8)]
                for a in range(GROUP)
            ]
            small = [
                [jnp.broadcast_to(line[a][:, k + c : k + c + 1], wide) for c in range(a + 1)] for a in range(GROUP)
            ]
            for c in range(GROUP):
                root = lax.rsqrt(small[c][c])
                line[c] = line[c] * root
                side[c] = [v * root for v in side[c]]
                factor = [small[a][c] * root for a in range(c + 1, GROUP)]
                for a in range(c + 1, GROUP):
                    f = factor[a - c - 1]
                    line[a] = line[a] - f * line[c]
                    side[a] = [v - f * w for v, w in zip(side[a], side[c])]
                    for e in range(c + 1, a + 1):
                        small[a][e] = small[a][e] - f * factor[e - c - 1]
            if at == 0:
                done[m].append(line[0])
            for a in range(GROUP):
                done[m][first] = jnp.where(sub == at + a, line[a], done[m][first])
            stay = first + (at + GROUP == 8)
            for t in range(stay, size // 8):
                for a in range(GROUP):
                    tiles[t] = tiles[t] - side[a][t - first] * line[a]
    return [jnp.concatenate(d, axis=0)[:, size:] for d in done]


def basis_kernel(
    own, place, row_terms, col_terms, omega_ref, psi_ref, weight_ref, row_ref, col_ref, aug
):
    width = omega_ref.shape[2]
    height = omega_ref.shape[1]
    for k in range(own):
        scale = weight_ref[pl.ds(place[0] * own + k, 1), :]
        for p in range(height // LANES):
            span = slice(p * LANES, (p + 1) * LANES)
            tile = upright(scale[:, span])
            for half in range(width // LANES):
                lanes = slice(half * LANES, (half + 1) * LANES)
                row_ref[k, span, lanes] = tile * omega_ref[k, span, lanes]
                col_ref[k, span, lanes] = tile * psi_ref[k, span, lanes]
        for terms, out in ((row_terms, row_ref), (col_terms, col_ref)):
            part = terms.shape[2]
            for c in range(terms.shape[0]):
                span = slice(c * part, (c + 1) * part)
                out[k, span, :] += terms[c, k]
    rows = lax.broadcasted_iota(jnp.int32, (width, width), 0)
    cols = lax.broadcasted_iota(jnp.int32, (width, width), 1)
    eye = (rows == cols).astype(jnp.float32)
    sources = [(out, k) for k in range(own) for out in (row_ref, col_ref)]
    for m, (out, k) in enumerate(sources):
        aug[m, :, :width] = dot(out[k], out[k], ((0,), (0,)))
        aug[m, :, width:] = eye
    steps = width // BASE
    lane = lax.broadcasted_iota(jnp.int32, (BASE, width), 1)
    for s in range(steps):
        span = slice(s * BASE, (s + 1) * BASE)
        inverses = invert_base([aug[m, span, span] for m in range(len(sources))])
        for m in range(len(sources)):
            panel = dot(inverses[m], aug[m, span, :], ((1,), (0,)))
            aug[m, span, :] = panel
            if s + 1 < steps:
                rest = slice((s + 1) * BASE, width)
                update = dot(jnp.where(lane >= (s + 1) * BASE, panel[:, :width], 0.0), panel, ((0,), (0,)))
                aug[m, rest, :] = aug[m, rest, :] - update[(s + 1) * BASE :]
    for m, (out, k) in enumerate(sources):
        out[k] = dot(out[k], aug[m, :, width:], ((1,), (1,)))


def move_psi(psi, own, ratio, row, col, n_row, n_col):
    first = lax.rem(col, ratio) * (own * n_row)
    result = None
    home = col // ratio
    for shift in range(n_row):
        target = lax.rem(home + shift, n_row)
        piece = lax.dynamic_slice_in_dim(psi, first + target * own, own, 0)
        if shift:
            pairs = [
                ((c // ratio) * n_col + c, ((c // ratio + shift) % n_row) * n_col + c) for c in range(n_col)
            ]
            piece = lax.ppermute(piece, ("row", "col"), pairs)
        result = piece if result is None else jnp.where(row == target, piece, result)
    return result


def per_device(positions, modulus, self_weight, omega, psi, blocks, *, n_row, n_col):
    col_clusters, height, width = omega.shape
    row_clusters = psi.shape[0]
    zones = positions.shape[1] // col_clusters
    ratio = row_clusters // col_clusters
    own = col_clusters // n_row
    row = lax.axis_index("row")
    col = lax.axis_index("col")
    pairs = blocks.reshape(-1, 2)
    slots = pairs.shape[0]

    points = jnp.concatenate([positions, modulus[None]], axis=0)
    meta = jnp.pad(pairs.astype(jnp.float32).reshape(1, -1), ((0, 7), (0, LANES - 2 * slots)))
    all_points, all_meta = remote_call(
        functools.partial(gather_kernel, (n_row, n_col, ratio)),
        [f32(n_col, 4, positions.shape[1]), f32(n_col + n_row, 8, LANES)],
        2 * n_col + n_row,
        2 * n_col + n_row,
        1,
        [points, meta],
    )
    all_points, all_meta, late_psi = lax.optimization_barrier((all_points, all_meta, psi))
    own_psi = move_psi(late_psi, own, ratio, row, col, n_row, n_col)
    metas = all_meta[:, 0, : 2 * slots].astype(jnp.int32).reshape(n_col + n_row, slots, 2)
    row_ids = metas[:n_col, :, 0].reshape(-1)
    col_ids = metas[n_col:, :, 1].reshape(-1)

    def table(lefts, rights, base, extra):
        at = jnp.where(lefts >= 0, lefts + base, -1)
        return jnp.stack([at, rights, jnp.broadcast_to(extra, at.shape)], axis=-1)

    row_base = (jnp.arange(n_row * slots, dtype=jnp.int32) // slots) * row_clusters
    row_table = table(metas[n_col:, :, 0].reshape(-1), col_ids, row_base, row)
    col_table = table(pairs[:, 0], pairs[:, 1], row * row_clusters, row)

    def left_map(n, ids):
        at = jnp.maximum(ids[n, 0], 0)
        return (at // col_clusters, 0, at % col_clusters)

    def term_call(kernel, count, rows, clusters_map, scratch, name):
        return pl.pallas_call(
            kernel,
            out_shape=f32(count, rows, width),
            grid_spec=pltpu.PrefetchScalarGridSpec(
                num_scalar_prefetch=1,
                grid=(count,),
                in_specs=[
                    pl.BlockSpec((1, 4, zones), left_map),
                    pl.BlockSpec((4, zones), lambda n, ids: (0, jnp.maximum(ids[n, 1], 0))),
                    pl.BlockSpec((1, height, width), clusters_map),
                ],
                out_specs=pl.BlockSpec((1, rows, width), lambda n, ids: (n, 0, 0)),
                scratch_shapes=scratch,
            ),
            cost_estimate=pl.CostEstimate(
                flops=12 * count * rows * height * width, bytes_accessed=8 * count * height * width, transcendentals=0
            ),
            name=name,
        )

    row_terms = term_call(
        row_terms_kernel,
        n_row * slots,
        height // n_row,
        lambda n, ids: (jnp.maximum(ids[n, 1], 0), 0, 0),
        [pltpu.VMEM((4, zones, zones), jnp.float32)],
        "row_terms",
    )(row_table, all_points, points, omega)
    col_terms = term_call(
        col_terms_kernel,
        slots,
        height,
        lambda n, ids: (lax.rem(jnp.maximum(ids[n, 0], 0), row_clusters), 0, 0),
        [],
        "col_terms",
    )(col_table, all_points, points, psi)

    sizes = (n_row, n_col, ratio, own)
    row_part = height // n_col
    col_part = height // n_row
    got_rows, got_cols = remote_call(
        functools.partial(spread_kernel, sizes),
        [f32(n_col, slots, row_part, width), f32(n_row, slots, col_part, width)],
        n_col + n_row,
        n_col + n_row,
        2,
        [row_terms.reshape(n_row, slots, height // n_row, width), col_terms],
    )
    row_chunks, col_chunks = sum_terms(row_ids, col_ids, got_rows, got_cols, row_clusters, col_clusters)
    full_rows, full_cols = remote_call(
        functools.partial(collect_kernel, sizes),
        [f32(n_col, own, row_part, width), f32(n_row, own, col_part, width)],
        n_col + n_row,
        n_col + n_row,
        3,
        [row_chunks, col_chunks],
    )

    def whole(shape):
        return pl.BlockSpec(shape, lambda n, _: (0,) * len(shape), pipeline_mode=pl.Buffered(1))

    row_basis, col_basis = pl.pallas_call(
        functools.partial(basis_kernel, own),
        out_shape=[f32(own, height, width), f32(own, height, width)],
        grid_spec=pltpu.PrefetchScalarGridSpec(
            num_scalar_prefetch=1,
            grid=(1,),
            in_specs=[
                whole(full_rows.shape),
                whole(full_cols.shape),
                pl.BlockSpec((own, height, width), lambda n, at: (at[0], 0, 0), pipeline_mode=pl.Buffered(1)),
                whole(own_psi.shape),
                whole(self_weight.shape),
            ],
            out_specs=[whole(own_psi.shape), whole(own_psi.shape)],
            scratch_shapes=[pltpu.VMEM((2 * own, width, 2 * width), jnp.float32)],
        ),
        name="basis",
    )(row.astype(jnp.int32)[None], full_rows, full_cols, omega, own_psi, self_weight)
    return tuple(
        remote_call(
            functools.partial(deliver_kernel, sizes),
            [f32(row_clusters, row_part, width), f32(col_clusters, col_part, width)],
            n_col + n_row,
            n_col + n_row,
            4,
            [row_basis, col_basis],
        )
    )


def solution(mesh):
    placed = (
        P(None, "col"),
        P("col"),
        P("col", None),
        P("col", None, None),
        P("row", None, None),
        P("row", "col", None, None),
    )
    return jax.shard_map(
        functools.partial(per_device, n_row=mesh.shape["row"], n_col=mesh.shape["col"]),
        mesh=mesh,
        in_specs=placed,
        out_specs=(P("row", "col", None), P("col", "row", None)),
        check_vma=False,
    )
```
